512 devices in a mesh: dp: 4 (over z_lo), context: 128 (over x, z_hi, y, core).
Axes of the slice: x: 4, y: 8, z: 8 (z_hi: 2, z_lo: 4; z = z_hi * 4 + z_lo), core: 2. Of those that a mesh axis runs over, the one named last changes fastest.
Arguments:
- projected: bfloat16 [3, 16384, 8192], P(None, 'context', 'dp'), parts along dimension 2, may hold values from -6 to 6
- conv_weight: float32 [3, 3, 8192], P(None, None, 'dp'), parts along dimension 2, may hold values from -3 to 3
- bias: float32 [8192], P('dp'), parts along dimension 0, may hold values from -4 to 4
- spectrum: float32 [2, 256, 128, 512], P(None, 'context', None, 'dp'), parts along dimension 3, as said below
Outputs:
- block_out: float32 [16384, 8192], P('context', 'dp'), parts along dimension 1
The draws below stay inside these ranges and needn't reach their ends.
There are 4 independent parts, one for each index of `dp`. The reference program is written for one: setup_inputs(seed, part) draws one part's arguments, and reference() takes and returns one part's arrays. A program takes and returns all parts, laid end to end along the dimension named above; each array names one. Nothing has to cross between parts.
Inputs may be any that keep to these rules, and one draw needn't show every extreme that they name: `spectrum`: each filter is real: for every k, entry k of the real part equals entry (32768 - k) mod 32768, and entry k of the imaginary part is the negative of that entry (frequency k stored at [., k mod 256, k // 256, .]).
All inputs are finite; a program needn't handle non-finite values.
Results may differ from the reference program's by a relative error of at most 0.0045.
Values may be sent and summed in bfloat16 or wider, within the bound.
A program may use at most 64 MiB of HBM per device.

```python
import jax
import jax.numpy as jnp
from jax import lax

COLS = 128
CH = 2048
FILTERS = 128
SEQ = 16384
ROWS = 256
FFTLEN = 32768


def draw_spectrum(key, part):
    sample = jax.random.normal(key, (2, FILTERS, FFTLEN), jnp.float32)
    mirror = jnp.roll(jnp.flip(sample, axis=-1), 1, axis=-1)
    real_part = (sample[0] + mirror[0]) * 0.7071
    imag_part = (sample[1] - mirror[1]) * 0.7071
    stacked = jnp.stack([real_part, imag_part])
    return jnp.transpose(stacked.reshape(2, FILTERS, COLS, ROWS), (0, 3, 2, 1))


def level_of(own_key, extent, pieces, least, high):
    factor_of, own = 1.0, jax.random.fold_in(own_key, 6)
    for axis_at, shards_of in pieces:
        steps = jnp.exp(jax.random.uniform(jax.random.fold_in(own, axis_at), (shards_of,), jnp.float32, least / len(pieces), high / len(pieces)))
        factor_of = factor_of * jnp.repeat(steps, extent[axis_at] // shards_of).reshape([-1 if axis == axis_at else 1 for axis in range(len(extent))])
    return factor_of


def normal_values(rng, extent, deviation, limit, split=(), kind=jnp.bfloat16):
    array = jax.random.normal(rng, extent, jnp.float32) * deviation
    if len(split) > 0:
        array = level_of(rng, extent, split, -0.22, 0.18) * array
    return jnp.clip(array, min=-limit, max=limit).astype(kind)


def setup_inputs(seed: int = 0, part: int = 0) -> dict:
    streams_of = jax.random.split(jax.random.key(seed), 5)
    part_splits = jax.random.split(jax.random.fold_in(streams_of[4], part), 5)
    return {
        "projected": normal_values(part_splits[0], (3, SEQ, CH), 1.0, 6.0, ((1, 128),)),
        "conv_weight": normal_values(part_splits[1], (3, 3, CH), 0.5, 3.0, (), jnp.float32),
        "bias": normal_values(part_splits[2], (CH,), 1.0, 4.0, (), jnp.float32),
        "spectrum": draw_spectrum(jax.random.fold_in(jax.random.fold_in(streams_of[4], part), 71), part),
    }


def reference(projected, conv_weight, bias, spectrum):
    signal_in = projected.astype(jnp.float32)
    padded = jnp.pad(signal_in, ((0, 0), (2, 0), (0, 0)))
    shorts = (conv_weight[:, 0:1, :] * padded[:, 2:, :]
              + conv_weight[:, 1:2, :] * padded[:, 1:-1, :]
              + conv_weight[:, 2:3, :] * padded[:, :-2, :])
    gated = (shorts[1] * shorts[2]).astype(jnp.bfloat16)
    gated_f = gated.astype(jnp.float32)
    fft_len = 2 * SEQ
    gated_t = jnp.transpose(gated_f).reshape(FILTERS, 16, SEQ)
    filt = spectrum[0] + 1j * spectrum[1]
    filt = jnp.transpose(filt, (2, 1, 0)).reshape(FILTERS, fft_len)

    def one_filter(item):
        signal, filter_row = item
        freq_in = jnp.fft.fft(signal, n=fft_len, axis=-1)
        return jnp.fft.ifft(freq_in * filter_row[None, :], axis=-1)[:, :SEQ].real

    long_conv = lax.map(one_filter, (gated_t, filt))
    long_conv = jnp.transpose(long_conv.reshape(CH, SEQ))
    return shorts[0] * (long_conv + bias[None, :] * gated_f)
```

```python
import math

import jax
import jax.numpy as jnp
import numpy as np
from jax import lax
from jax.sharding import PartitionSpec as P

COLS = 128
SHARE = 16
HIGHEST = lax.Precision.HIGHEST


def tables(data_rows):
    grid_rows = 2 * data_rows
    fft_len = grid_rows * COLS
    c = np.arange(grid_rows)
    a = np.arange(data_rows)
    b = np.arange(COLS)
    rows = 2.0 * np.pi * (np.outer(c, a) % grid_rows) / grid_rows
    cols = 2.0 * np.pi * (np.outer(b, b) % COLS) / COLS
    twist = 2.0 * np.pi * (np.outer(c, b) % fft_len) / fft_len
    rc, rs = np.cos(rows), np.sin(rows)
    cc, cs = np.cos(cols), np.sin(cols)
    first = np.block([[rc, rs], [-rs, rc]])
    mid = np.block([[cc, -cs], [cs, cc]])
    back = np.block([[cc, cs], [-cs, cc]])
    last = np.block([[rc.T, -rs.T], [rs.T, rc.T]]) / fft_len
    made = (first, mid, back, last, np.cos(twist), np.sin(twist))
    return tuple(t.astype(np.float32) for t in made)


def from_behind(shard, axis, by):
    devices = lax.axis_size(axis)
    pairs = [(i, i + by) for i in range(devices) if 0 <= i + by < devices]
    return lax.ppermute(shard, axis, pairs)


def local(projected, conv_weight, bias, spectrum):
    group = lax.axis_size("context")
    local_len = projected.shape[1]
    channels = projected.shape[2]
    half = SHARE // 2
    grid_rows = 2 * group
    left_rim = from_behind(projected[:, local_len - 2 :, :], "context", 1)
    extended = jnp.concatenate([left_rim, projected], axis=1).astype(jnp.float32)
    shorts = (
        conv_weight[:, 0:1, :] * extended[:, 2:, :]
        + conv_weight[:, 1:2, :] * extended[:, 1:-1, :]
        + conv_weight[:, 2:3, :] * extended[:, :-2, :]
    )
    gated = (shorts[1] * shorts[2]).astype(jnp.bfloat16)
    signal = jnp.transpose(gated).reshape(group, SHARE, COLS)
    filters = jnp.transpose(spectrum.astype(jnp.bfloat16), (3, 0, 1, 2)).reshape(group, 4, COLS)
    sent = jnp.concatenate([signal, filters], axis=1)
    held = lax.all_to_all(sent, "context", split_axis=0, concat_axis=0, tiled=True)
    first, mid, back, last, twist_cos, twist_sin = tables(group)
    x = held[:, :SHARE, :].astype(jnp.float32)
    f = held[:, SHARE:, :].astype(jnp.float32).reshape(group, 2, 2, COLS)
    fr = f[:, 0].reshape(grid_rows, 1, COLS)
    fi = f[:, 1].reshape(grid_rows, 1, COLS)
    x = jnp.concatenate([x[:, :half], x[:, half:]], axis=0)
    tc, ts = twist_cos[:, None, :], twist_sin[:, None, :]
    y = jnp.einsum("ca,ahb->chb", first, x, precision=HIGHEST)
    yr, yi = y[:grid_rows], y[grid_rows:]
    z = jnp.concatenate([yr * tc + yi * ts, yi * tc - yr * ts], axis=2)
    g = jnp.einsum("chb,bd->chd", z, mid, precision=HIGHEST)
    gr, gi = g[:, :, :COLS], g[:, :, COLS:]
    p = jnp.concatenate([gr * fr - gi * fi, gr * fi + gi * fr], axis=2)
    q = jnp.einsum("chd,db->chb", p, back, precision=HIGHEST)
    qr, qi = q[:, :, :COLS], q[:, :, COLS:]
    r = jnp.concatenate([qr * tc - qi * ts, qi * tc + qr * ts], axis=0)
    out = jnp.einsum("ac,chb->ahb", last, r, precision=HIGHEST)
    out = jnp.concatenate([out[:group], out[group:]], axis=1).astype(jnp.bfloat16)
    conv = lax.all_to_all(out, "context", split_axis=0, concat_axis=0, tiled=True)
    long_conv = jnp.transpose(conv.reshape(channels, local_len)).astype(jnp.float32)
    return shorts[0] * (long_conv + bias[None, :] * gated.astype(jnp.float32))


def solution(mesh):
    placed = (
        P(None, "context", "dp"),
        P(None, None, "dp"),
        P("dp"),
        P(None, "context", None, "dp"),
    )
    return jax.shard_map(
        local, mesh=mesh, in_specs=placed, out_specs=P("context", "dp"), check_vma=False
    )
```

```python
import functools

import jax
import jax.numpy as jnp
import numpy as np
from jax import lax
from jax.experimental import pallas as pl
from jax.experimental.pallas import tpu as pltpu
from jax.sharding import PartitionSpec as P

COLS = 128
SHARE = 16
HALF = SHARE // 2


def tables(data_rows):
    grid_rows = 2 * data_rows
    fft_len = grid_rows * COLS
    c = np.concatenate([np.arange(0, grid_rows, 2), np.arange(1, grid_rows, 2)])
    a = np.arange(data_rows)
    b = np.arange(COLS)
    rows = 2.0 * np.pi * (np.outer(c, a) % grid_rows) / grid_rows
    cols = 2.0 * np.pi * (np.outer(b, b) % COLS) / COLS
    twist = 2.0 * np.pi * (np.outer(c, b) % fft_len) / fft_len
    rc, rs = np.cos(rows), np.sin(rows)
    cc, cs = np.cos(cols), np.sin(cols)
    first = np.block([[rc, rs], [-rs, rc]])
    mid = np.block([[cc, -cs], [cs, cc]])
    back = np.block([[cc, cs], [-cs, cc]])
    last = np.block([[rc.T, -rs.T], [rs.T, rc.T]]) / fft_len
    split = []
    for table in (first, mid, back, last):
        table = table.astype(np.float32)
        high = table.astype(jnp.bfloat16)
        split += [high, (table - high.astype(np.float32)).astype(jnp.bfloat16)]
    return split + [np.cos(twist).astype(np.float32), np.sin(twist).astype(np.float32)]


def mm(x, y):
    return jnp.dot(x, y, preferred_element_type=jnp.float32)


def halves(x):
    high = x.astype(jnp.bfloat16)
    return high, (x - high.astype(jnp.float32)).astype(jnp.bfloat16)


def transform(xs, sp, ys, tabs):
    fh, fl, mh, ml, bh, bl, lh, ll, tc_ref, ts_ref = tabs
    tc, ts = tc_ref[...], ts_ref[...]
    grid_rows = tc.shape[0]
    fr = jnp.concatenate([sp[:, 0, :], sp[:, 1, :]], axis=0)
    fi = jnp.concatenate([sp[:, 2, :], sp[:, 3, :]], axis=0)
    for h in range(0, HALF, 2):
        pair = [
            jnp.concatenate([xs[:, i, :], xs[:, i + HALF, :]], axis=0).astype(jnp.bfloat16)
            for i in (h, h + 1)
        ]
        x = jnp.concatenate(pair, axis=1)
        y = mm(fh[...], x) + mm(fl[...], x)
        turned = []
        for i in range(2):
            yr = y[:grid_rows, i * COLS : (i + 1) * COLS]
            yi = y[grid_rows:, i * COLS : (i + 1) * COLS]
            zh, zl = halves(jnp.concatenate([yr * tc + yi * ts, yi * tc - yr * ts], axis=1))
            g = mm(zh, mh[...]) + mm(zl, mh[...]) + mm(zh, ml[...])
            gr, gi = g[:, :COLS], g[:, COLS:]
            ph, plo = halves(jnp.concatenate([gr * fr - gi * fi, gr * fi + gi * fr], axis=1))
            q = mm(ph, bh[...]) + mm(plo, bh[...]) + mm(ph, bl[...])
            qr, qi = q[:, :COLS], q[:, COLS:]
            turned.append(jnp.concatenate([qr * tc - qi * ts, qi * tc + qr * ts], axis=0))
        rh, rl = halves(jnp.concatenate(turned, axis=1))
        o = mm(lh[...], rh) + mm(lh[...], rl) + mm(ll[...], rh)
        n = grid_rows // 2
        for i in range(2):
            ys[:, h + i, :] = o[:n, i * COLS : (i + 1) * COLS]
            ys[:, h + i + HALF, :] = o[n:, i * COLS : (i + 1) * COLS]


def kernel(group, proj, weight, bias, spec, *refs):
    tabs = refs[:10]
    out = refs[10]
    (tail, halo, q_keep, gated, xs, ys, sf, sig_out, sig_in, spec_out, spec_in, conv_out, conv_in,
     send_sems, recv_sems, own_sems) = refs[11:]
    me = lax.axis_index("context")
    rows = proj.shape[1]
    blocks = proj.shape[2] // COLS
    per = COLS // SHARE

    def copy_to(src, dst, number, peer):
        return pltpu.make_async_remote_copy(
            src_ref=src,
            dst_ref=dst,
            send_sem=send_sems.at[number],
            recv_sem=recv_sems.at[number],
            device_id={"context": peer},
            device_id_type=pl.DeviceIdType.MESH,
        )

    def await_all(src, dst, number):
        some = pl.ds(0, group - 1)
        pltpu.make_async_copy(src.at[some], dst.at[some], send_sems.at[number]).wait()
        pltpu.make_async_copy(src.at[some], dst.at[some], recv_sems.at[number]).wait()

    halo[...] = jnp.zeros_like(halo)
    barrier = pltpu.get_barrier_semaphore()

    @pl.loop(1, group)
    def _(k):
        pl.semaphore_signal(
            barrier,
            inc=1,
            device_id={"context": lax.rem(me + k, group)},
            device_id_type=pl.DeviceIdType.MESH,
        )

    ends = [proj[j, rows - 16 :, :].astype(jnp.float32)[14:16, :] for j in range(3)]
    ends.append(jnp.zeros_like(ends[0]))
    tail[...] = jnp.concatenate(ends, axis=0).astype(jnp.bfloat16)
    for i in range(2):
        for j in range(2):
            sf[:, 2 * i + j, :] = jnp.transpose(spec[i, j])
    spec_out[...] = sf[...].astype(jnp.bfloat16)
    pl.semaphore_wait(barrier, group - 1)

    @pl.when(me < group - 1)
    def _():
        copy_to(tail, halo, 0, me + 1).start()

    own_spec = pltpu.make_async_copy(spec_out.at[me], spec_in.at[me], own_sems.at[0])
    own_spec.start()

    @pl.loop(1, group)
    def _(k):
        peer = lax.rem(me + k, group)
        copy_to(spec_out.at[peer], spec_in.at[me], 1, peer).start()

    @pl.when(me > 0)
    def _():
        copy_to(tail, halo, 0, me).wait_recv()

    @pl.when(me < group - 1)
    def _():
        copy_to(tail, halo, 0, me).wait_send()

    row = lax.broadcasted_iota(jnp.int32, (rows, COLS), 0)

    @pl.loop(0, blocks)
    def _(step):
        block = lax.rem(step + me // per, blocks)
        lanes = pl.ds(pl.multiple_of(block * COLS, COLS), COLS)
        edge = halo[:, lanes].astype(jnp.float32)
        shorts = []
        for j in range(3):
            x = proj[j, :, lanes].astype(jnp.float32)
            e2, e1 = edge[2 * j : 2 * j + 1, :], edge[2 * j + 1 : 2 * j + 2, :]
            x1 = jnp.where(row == 0, e1, pltpu.roll(x, 1, 0))
            x2 = jnp.where(row == 0, e2, jnp.where(row == 1, e1, pltpu.roll(x, 2, 0)))
            w = weight[j, :, lanes]
            shorts.append(w[0:1] * x + w[1:2] * x1 + w[2:3] * x2)
        q_keep[:, lanes] = shorts[0]
        g = (shorts[1] * shorts[2]).astype(jnp.bfloat16)
        gated[:, lanes] = g
        turned = jnp.transpose(g.astype(jnp.float32)).astype(jnp.bfloat16)
        sig_out[pl.ds(block * per, per)] = turned.reshape(per, SHARE, COLS)

    own_sig = pltpu.make_async_copy(sig_out.at[me], sig_in.at[me], own_sems.at[1])
    own_sig.start()

    @pl.loop(1, group)
    def _(k):
        peer = lax.rem(me + k, group)
        copy_to(sig_out.at[peer], sig_in.at[me], 2, peer).start()

    await_all(spec_out, spec_in, 1)
    own_spec.wait()
    sf[...] = spec_in[...].astype(jnp.float32)
    await_all(sig_out, sig_in, 2)
    own_sig.wait()
    xs[...] = sig_in[...].astype(jnp.float32)
    transform(xs, sf, ys, tabs)
    conv_out[...] = ys[...].astype(jnp.bfloat16)

    own_conv = pltpu.make_async_copy(conv_out.at[me], conv_in.at[me], own_sems.at[2])
    own_conv.start()

    @pl.loop(1, group)
    def _(k):
        peer = lax.rem(me + k, group)
        copy_to(conv_out.at[peer], conv_in.at[me], 3, peer).start()

    await_all(conv_out, conv_in, 3)
    own_conv.wait()

    @pl.loop(0, blocks)
    def _(block):
        lanes = pl.ds(pl.multiple_of(block * COLS, COLS), COLS)
        conv = conv_in[pl.ds(block * per, per)].reshape(COLS, COLS).astype(jnp.float32)
        skip = bias[:, lanes] * gated[:, lanes].astype(jnp.float32)
        out[:, lanes] = q_keep[:, lanes] * (jnp.transpose(conv) + skip)


def local(projected, conv_weight, bias, spectrum):
    group = lax.axis_size("context")
    rows, channels = projected.shape[1:]
    bf16, f32 = jnp.bfloat16, jnp.float32
    made = tables(group)
    vmem = pl.BlockSpec(memory_space=pltpu.VMEM)
    return pl.pallas_call(
        functools.partial(kernel, group),
        out_shape=jax.ShapeDtypeStruct((rows, channels), f32),
        in_specs=[vmem] * (4 + len(made)),
        out_specs=vmem,
        scratch_shapes=[
            pltpu.VMEM((8, channels), bf16),
            pltpu.VMEM((8, channels), bf16),
            pltpu.VMEM((rows, channels), f32),
            pltpu.VMEM((rows, channels), bf16),
            pltpu.VMEM((group, SHARE, COLS), f32),
            pltpu.VMEM((group, SHARE, COLS), f32),
            pltpu.VMEM((group, 4, COLS), f32),
            pltpu.VMEM((group, SHARE, COLS), bf16),
            pltpu.VMEM((group, SHARE, COLS), bf16),
            pltpu.VMEM((group, 4, COLS), bf16),
            pltpu.VMEM((group, 4, COLS), bf16),
            pltpu.VMEM((group, SHARE, COLS), bf16),
            pltpu.VMEM((group, SHARE, COLS), bf16),
            pltpu.SemaphoreType.DMA((4,)),
            pltpu.SemaphoreType.DMA((4,)),
            pltpu.SemaphoreType.DMA((3,)),
        ],
        compiler_params=pltpu.CompilerParams(collective_id=0, has_side_effects=True),
        name="hyena",
    )(projected, conv_weight, bias[None, :], spectrum, *made)


def solution(mesh):
    placed = (
        P(None, "context", "dp"),
        P(None, None, "dp"),
        P("dp"),
        P(None, "context", None, "dp"),
    )
    return jax.shard_map(
        local, mesh=mesh, in_specs=placed, out_specs=P("context", "dp"), check_vma=False
    )
```

```python
import functools

import jax
import jax.numpy as jnp
import numpy as np
from jax import lax
from jax.experimental import pallas as pl
from jax.experimental.pallas import tpu as pltpu
from jax.sharding import PartitionSpec as P

COLS = 128
SHARE = 16
PARTS = 2
PIECE = SHARE // PARTS
HALF = PIECE // 2


def tables(data_rows):
    grid_rows = 2 * data_rows
    fft_len = grid_rows * COLS
    c = np.concatenate([np.arange(0, grid_rows, 2), np.arange(1, grid_rows, 2)])
    a = np.arange(data_rows)
    b = np.arange(COLS)
    rows = 2.0 * np.pi * (np.outer(c, a) % grid_rows) / grid_rows
    cols = 2.0 * np.pi * (np.outer(b, b) % COLS) / COLS
    twist = 2.0 * np.pi * (np.outer(c, b) % fft_len) / fft_len
    rc, rs = np.cos(rows), np.sin(rows)
    cc, cs = np.cos(cols), np.sin(cols)
    first = np.block([[rc, rs], [-rs, rc]])
    mid = np.block([[cc, -cs], [cs, cc]])
    back = np.block([[cc, cs], [-cs, cc]])
    last = np.block([[rc.T, -rs.T], [rs.T, rc.T]]) / fft_len
    split = []
    for table in (first, mid, back, last):
        table = table.astype(np.float32)
        high = table.astype(jnp.bfloat16)
        split += [high, (table - high.astype(np.float32)).astype(jnp.bfloat16)]
    return split + [np.cos(twist).astype(np.float32), np.sin(twist).astype(np.float32)]


def mm(x, y):
    return jnp.dot(x, y, preferred_element_type=jnp.float32)


def transform(xs, sp, ys, tabs):
    fh, fl, mh, ml, bh, bl, lh, ll, tc_ref, ts_ref = tabs
    tc, ts = tc_ref[...], ts_ref[...]
    grid_rows = tc.shape[0]
    fr = jnp.concatenate([sp[:, 0, :], sp[:, 1, :]], axis=0)
    fi = jnp.concatenate([sp[:, 2, :], sp[:, 3, :]], axis=0)
    for h in range(0, HALF, 2):
        pair = [
            jnp.concatenate([xs[:, i, :], xs[:, i + HALF, :]], axis=0).astype(jnp.bfloat16)
            for i in (h, h + 1)
        ]
        x = jnp.concatenate(pair, axis=1)
        y = mm(fh[...], x) + mm(fl[...], x)
        turned = []
        for i in range(2):
            yr = y[:grid_rows, i * COLS : (i + 1) * COLS]
            yi = y[grid_rows:, i * COLS : (i + 1) * COLS]
            z = jnp.concatenate([yr * tc + yi * ts, yi * tc - yr * ts], axis=1)
            z = z.astype(jnp.bfloat16)
            g = mm(z, mh[...]) + mm(z, ml[...])
            gr, gi = g[:, :COLS], g[:, COLS:]
            p = jnp.concatenate([gr * fr - gi * fi, gr * fi + gi * fr], axis=1)
            p = p.astype(jnp.bfloat16)
            q = mm(p, bh[...]) + mm(p, bl[...])
            qr, qi = q[:, :COLS], q[:, COLS:]
            turned.append(jnp.concatenate([qr * tc - qi * ts, qi * tc + qr * ts], axis=0))
        r = jnp.concatenate(turned, axis=1).astype(jnp.bfloat16)
        o = mm(lh[...], r) + mm(ll[...], r)
        n = grid_rows // 2
        for i in range(2):
            ys[:, h + i, :] = o[:n, i * COLS : (i + 1) * COLS]
            ys[:, h + i + HALF, :] = o[n:, i * COLS : (i + 1) * COLS]


def kernel(group, proj, weight, bias, spec, *refs):
    tabs = refs[:10]
    q_keep, total = refs[10:12]
    (tail, halo, gated, xs, ys, sf, sig_out, sig_in, spec_out, spec_in, conv_out, conv_in,
     send_sems, recv_sems, own_sems) = refs[12:]
    me = lax.axis_index("context")
    rows = proj.shape[1]
    blocks = proj.shape[2] // COLS
    per = COLS // SHARE

    def copy_to(src, dst, number, peer):
        return pltpu.make_async_remote_copy(
            src_ref=src,
            dst_ref=dst,
            send_sem=send_sems.at[number],
            recv_sem=recv_sems.at[number],
            device_id={"context": peer},
            device_id_type=pl.DeviceIdType.MESH,
        )

    def all_copies(src, dst, sem):
        some = pl.ds(0, group - 1)
        return pltpu.make_async_copy(src.at[some], dst.at[some], sem)

    def keep(src, dst, number):
        return pltpu.make_async_copy(src.at[me], dst.at[me], own_sems.at[number])

    def to_all(src, dst, number):
        @pl.loop(1, group)
        def _(k):
            peer = lax.rem(me + k, group)
            copy_to(src.at[peer], dst.at[me], number, peer).start()

    halo[...] = jnp.zeros_like(halo)
    barrier = pltpu.get_barrier_semaphore()

    @pl.loop(1, group)
    def _(k):
        pl.semaphore_signal(
            barrier,
            inc=1,
            device_id={"context": lax.rem(me + k, group)},
            device_id_type=pl.DeviceIdType.MESH,
        )

    ends = [proj[j, rows - 16 :, :].astype(jnp.float32)[14:16, :] for j in range(3)]
    ends.append(jnp.zeros_like(ends[0]))
    tail[...] = jnp.concatenate(ends, axis=0).astype(jnp.bfloat16)
    for i in range(2):
        for j in range(2):
            sf[:, 2 * i + j, :] = jnp.transpose(spec[i, j])
    spec_out[...] = sf[...].astype(jnp.bfloat16)
    pl.semaphore_wait(barrier, group - 1)

    @pl.when(me < group - 1)
    def _():
        copy_to(tail, halo, 0, me + 1).start()

    own_spec = keep(spec_out, spec_in, 0)
    own_spec.start()

    to_all(spec_out, spec_in, 1)

    @pl.when(me > 0)
    def _():
        copy_to(tail, halo, 0, me).wait_recv()

    @pl.when(me < group - 1)
    def _():
        copy_to(tail, halo, 0, me).wait_send()

    def send_block(block):
        for i in range(per):
            peer = block * per + lax.rem(me + i, per)

            @pl.when(peer != me)
            def _():
                copy_to(sig_out.at[0, peer], sig_in.at[0, me], 2, peer).start()

    row = lax.broadcasted_iota(jnp.int32, (rows, COLS), 0)

    @pl.loop(0, blocks)
    def _(step):
        block = lax.rem(step + me // per, blocks)
        lanes = pl.ds(pl.multiple_of(block * COLS, COLS), COLS)
        edge = halo[:, lanes].astype(jnp.float32)
        shorts = []
        for j in range(3):
            x = proj[j, :, lanes].astype(jnp.float32)
            e2, e1 = edge[2 * j : 2 * j + 1, :], edge[2 * j + 1 : 2 * j + 2, :]
            x1 = jnp.where(row == 0, e1, pltpu.roll(x, 1, 0))
            x2 = jnp.where(row == 0, e2, jnp.where(row == 1, e1, pltpu.roll(x, 2, 0)))
            w = weight[j, :, lanes]
            shorts.append(w[0:1] * x + w[1:2] * x1 + w[2:3] * x2)
        q_keep[:, lanes] = shorts[0]
        g = (shorts[1] * shorts[2]).astype(jnp.bfloat16)
        gated[:, lanes] = g
        turned = jnp.transpose(g.astype(jnp.float32))
        turned = turned.reshape(per, PARTS, PIECE, COLS)
        for part in range(PARTS):
            sig_out[part, pl.ds(block * per, per)] = turned[:, part].astype(jnp.bfloat16)

        @pl.when(step > 0)
        def _():
            send_block(lax.rem(step + blocks - 1 + me // per, blocks))

    send_block(lax.rem(blocks - 1 + me // per, blocks))
    for part in range(PARTS):
        keep(sig_out.at[part], sig_in.at[part], 1 + part).start()
    for part in range(1, PARTS):
        to_all(sig_out.at[part], sig_in.at[part], 2 + part)

    all_copies(spec_out, spec_in, recv_sems.at[1]).wait()
    own_spec.wait()
    sf[...] = spec_in[...].astype(jnp.float32)
    for part in range(PARTS):
        all_copies(sig_out.at[part], sig_in.at[part], recv_sems.at[2 + part]).wait()
        keep(sig_out.at[part], sig_in.at[part], 1 + part).wait()
        xs[...] = sig_in[part].astype(jnp.float32)
        transform(xs, sf, ys, tabs)
        conv_out[part] = ys[...].astype(jnp.bfloat16)
        keep(conv_out.at[part], conv_in.at[part], 1 + PARTS + part).start()
        to_all(conv_out.at[part], conv_in.at[part], 2 + PARTS + part)

    all_copies(spec_out, spec_in, send_sems.at[1]).wait()
    for part in range(PARTS):
        all_copies(sig_out.at[part], sig_in.at[part], send_sems.at[2 + part]).wait()
    for part in range(PARTS):
        number = 2 + PARTS + part
        all_copies(conv_out.at[part], conv_in.at[part], send_sems.at[number]).wait()
        all_copies(conv_out.at[part], conv_in.at[part], recv_sems.at[number]).wait()
        keep(conv_out.at[part], conv_in.at[part], 1 + PARTS + part).wait()

    @pl.loop(0, blocks)
    def _(block):
        lanes = pl.ds(pl.multiple_of(block * COLS, COLS), COLS)
        pieces = [
            conv_in[part, pl.ds(block * per, per)].astype(jnp.float32)[:, None]
            for part in range(PARTS)
        ]
        conv = jnp.concatenate(pieces, axis=1).reshape(COLS, COLS)
        skip = bias[:, lanes] * gated[:, lanes].astype(jnp.float32)
        total[:, lanes] = jnp.transpose(conv) + skip


def local(projected, conv_weight, bias, spectrum):
    group = lax.axis_size("context")
    rows, channels = projected.shape[1:]
    bf16, f32 = jnp.bfloat16, jnp.float32
    made = tables(group)
    vmem = pl.BlockSpec(memory_space=pltpu.VMEM)
    q_short, total = pl.pallas_call(
        functools.partial(kernel, group),
        out_shape=[jax.ShapeDtypeStruct((rows, channels), f32)] * 2,
        in_specs=[vmem] * (4 + len(made)),
        out_specs=[vmem] * 2,
        scratch_shapes=[
            pltpu.VMEM((8, channels), bf16),
            pltpu.VMEM((8, channels), bf16),
            pltpu.VMEM((rows, channels), bf16),
            pltpu.VMEM((group, PIECE, COLS), f32),
            pltpu.VMEM((group, PIECE, COLS), f32),
            pltpu.VMEM((group, 4, COLS), f32),
            pltpu.VMEM((PARTS, group, PIECE, COLS), bf16),
            pltpu.VMEM((PARTS, group, PIECE, COLS), bf16),
            pltpu.VMEM((group, 4, COLS), bf16),
            pltpu.VMEM((group, 4, COLS), bf16),
            pltpu.VMEM((PARTS, group, PIECE, COLS), bf16),
            pltpu.VMEM((PARTS, group, PIECE, COLS), bf16),
            pltpu.SemaphoreType.DMA((2 + 2 * PARTS,)),
            pltpu.SemaphoreType.DMA((2 + 2 * PARTS,)),
            pltpu.SemaphoreType.DMA((1 + 2 * PARTS,)),
        ],
        compiler_params=pltpu.CompilerParams(collective_id=0, has_side_effects=True),
        name="hyena",
    )(projected, conv_weight, bias[None, :], spectrum, *made)
    return q_short * total


def solution(mesh):
    placed = (
        P(None, "context", "dp"),
        P(None, None, "dp"),
        P("dp"),
        P(None, "context", None, "dp"),
    )
    return jax.shard_map(
        local, mesh=mesh, in_specs=placed, out_specs=P("context", "dp"), check_vma=False
    )
```

```python
import functools

import jax
import jax.numpy as jnp
import numpy as np
from jax import lax
from jax.experimental import pallas as pl
from jax.experimental.pallas import tpu as pltpu
from jax.sharding import PartitionSpec as P

COLS = 128
SHARE = 16
PARTS = 4
PIECE = SHARE // PARTS
HALF = PIECE // 2


def tables(data_rows):
    grid_rows = 2 * data_rows
    fft_len = grid_rows * COLS
    c = np.concatenate([np.arange(0, grid_rows, 2), np.arange(1, grid_rows, 2)])
    a = np.arange(data_rows)
    b = np.arange(COLS)
    rows = 2.0 * np.pi * (np.outer(c, a) % grid_rows) / grid_rows
    cols = 2.0 * np.pi * (np.outer(b, b) % COLS) / COLS
    twist = 2.0 * np.pi * (np.outer(c, b) % fft_len) / fft_len
    rc, rs = np.cos(rows), np.sin(rows)
    cc, cs = np.cos(cols), np.sin(cols)
    first = np.block([[rc, rs], [-rs, rc]])
    mid = np.block([[cc, -cs], [cs, cc]])
    back = np.block([[cc, cs], [-cs, cc]])
    last = np.block([[rc.T, -rs.T], [rs.T, rc.T]]) / fft_len
    split = []
    for table in (first, mid, back, last):
        table = table.astype(np.float32)
        high = table.astype(jnp.bfloat16)
        split += [high, (table - high.astype(np.float32)).astype(jnp.bfloat16)]
    return split + [np.cos(twist).astype(np.float32), np.sin(twist).astype(np.float32)]


def mm(x, y):
    return jnp.dot(x, y, preferred_element_type=jnp.float32)


def transform(xs, sp, ys, tabs):
    fh, fl, mh, ml, bh, bl, lh, ll, tc_ref, ts_ref = tabs
    tc, ts = tc_ref[...], ts_ref[...]
    grid_rows = tc.shape[0]
    fr = jnp.concatenate([sp[:, 0, :], sp[:, 1, :]], axis=0)
    fi = jnp.concatenate([sp[:, 2, :], sp[:, 3, :]], axis=0)
    for h in range(0, HALF, 2):
        pair = [
            jnp.concatenate([xs[:, i, :], xs[:, i + HALF, :]], axis=0).astype(jnp.bfloat16)
            for i in (h, h + 1)
        ]
        x = jnp.concatenate(pair, axis=1)
        y = mm(fh[...], x) + mm(fl[...], x)
        turned = []
        for i in range(2):
            yr = y[:grid_rows, i * COLS : (i + 1) * COLS]
            yi = y[grid_rows:, i * COLS : (i + 1) * COLS]
            z = jnp.concatenate([yr * tc + yi * ts, yi * tc - yr * ts], axis=1)
            z = z.astype(jnp.bfloat16)
            g = mm(z, mh[...]) + mm(z, ml[...])
            gr, gi = g[:, :COLS], g[:, COLS:]
            p = jnp.concatenate([gr * fr - gi * fi, gr * fi + gi * fr], axis=1)
            p = p.astype(jnp.bfloat16)
            q = mm(p, bh[...]) + mm(p, bl[...])
            qr, qi = q[:, :COLS], q[:, COLS:]
            turned.append(jnp.concatenate([qr * tc - qi * ts, qi * tc + qr * ts], axis=0))
        r = jnp.concatenate(turned, axis=1).astype(jnp.bfloat16)
        o = mm(lh[...], r) + mm(ll[...], r)
        n = grid_rows // 2
        for i in range(2):
            ys[:, h + i, :] = o[:n, i * COLS : (i + 1) * COLS]
            ys[:, h + i + HALF, :] = o[n:, i * COLS : (i + 1) * COLS]


def kernel(group, proj, weight, bias, spec, *refs):
    tabs = refs[:10]
    out = refs[10]
    (tail, halo, q_keep, gated, xs, ys, sf, sig_out, sig_in, spec_out, spec_in, conv_out, conv_in,
     send_sems, recv_sems, own_sems) = refs[11:]
    me = lax.axis_index("context")
    rows = proj.shape[1]
    blocks = proj.shape[2] // COLS
    per = COLS // SHARE

    def copy_to(src, dst, number, peer):
        return pltpu.make_async_remote_copy(
            src_ref=src,
            dst_ref=dst,
            send_sem=send_sems.at[number],
            recv_sem=recv_sems.at[number],
            device_id={"context": peer},
            device_id_type=pl.DeviceIdType.MESH,
        )

    def all_copies(src, dst, sem):
        some = pl.ds(0, group - 1)
        return pltpu.make_async_copy(src.at[some], dst.at[some], sem)

    def keep(src, dst, number):
        return pltpu.make_async_copy(src.at[me], dst.at[me], own_sems.at[number])

    def to_all(src, dst, number):
        @pl.loop(1, group)
        def _(k):
            peer = lax.rem(me + k, group)
            copy_to(src.at[peer], dst.at[me], number, peer).start()

    halo[...] = jnp.zeros_like(halo)
    barrier = pltpu.get_barrier_semaphore()

    @pl.loop(1, group)
    def _(k):
        pl.semaphore_signal(
            barrier,
            inc=1,
            device_id={"context": lax.rem(me + k, group)},
            device_id_type=pl.DeviceIdType.MESH,
        )

    ends = [proj[j, rows - 16 :, :].astype(jnp.float32)[14:16, :] for j in range(3)]
    ends.append(jnp.zeros_like(ends[0]))
    tail[...] = jnp.concatenate(ends, axis=0).astype(jnp.bfloat16)
    for i in range(2):
        for j in range(2):
            sf[:, 2 * i + j, :] = jnp.transpose(spec[i, j])
    spec_out[...] = sf[...].astype(jnp.bfloat16)
    row = lax.broadcasted_iota(jnp.int32, (rows, COLS), 0)

    def short(x, j, lanes, e2, e1):
        n = row[: x.shape[0]]
        x1 = jnp.where(n == 0, e1, pltpu.roll(x, 1, 0))
        x2 = jnp.where(n == 0, e2, jnp.where(n == 1, e1, pltpu.roll(x, 2, 0)))
        w = weight[j, :, lanes]
        return w[0:1] * x + w[1:2] * x1 + w[2:3] * x2

    @pl.loop(0, blocks)
    def _(block):
        lanes = pl.ds(pl.multiple_of(block * COLS, COLS), COLS)
        none = jnp.zeros((1, COLS), jnp.float32)
        q, k, v = [
            short(proj[j, :, lanes].astype(jnp.float32), j, lanes, none, none) for j in range(3)
        ]
        q_keep[:, lanes] = q
        gated[:, lanes] = (k * v).astype(jnp.bfloat16)

    pl.semaphore_wait(barrier, group - 1)

    @pl.when(me < group - 1)
    def _():
        copy_to(tail, halo, 0, me + 1).start()

    own_spec = keep(spec_out, spec_in, 0)
    own_spec.start()

    to_all(spec_out, spec_in, 1)

    @pl.when(me > 0)
    def _():
        copy_to(tail, halo, 0, me).wait_recv()

    @pl.when(me < group - 1)
    def _():
        copy_to(tail, halo, 0, me).wait_send()

    def send_block(block):
        for i in range(per):
            peer = block * per + lax.rem(me + i, per)

            @pl.when(peer != me)
            def _():
                copy_to(sig_out.at[0, peer], sig_in.at[0, me], 2, peer).start()

    @pl.loop(0, blocks)
    def _(step):
        block = lax.rem(step + me // per, blocks)
        lanes = pl.ds(pl.multiple_of(block * COLS, COLS), COLS)
        edge = halo[:, lanes].astype(jnp.float32)
        q, k, v = [
            short(
                proj[j, 0:16, lanes].astype(jnp.float32),
                j,
                lanes,
                edge[2 * j : 2 * j + 1, :],
                edge[2 * j + 1 : 2 * j + 2, :],
            )
            for j in range(3)
        ]
        q_keep[0:16, lanes] = q
        gated[0:16, lanes] = (k * v).astype(jnp.bfloat16)
        turned = jnp.transpose(gated[:, lanes].astype(jnp.float32))
        turned = turned.reshape(per, PARTS, PIECE, COLS)
        for part in range(PARTS):
            sig_out[part, pl.ds(block * per, per)] = turned[:, part].astype(jnp.bfloat16)

        @pl.when(step > 0)
        def _():
            send_block(lax.rem(step + blocks - 1 + me // per, blocks))

    send_block(lax.rem(blocks - 1 + me // per, blocks))
    for part in range(PARTS):
        keep(sig_out.at[part], sig_in.at[part], 1 + part).start()
    for part in range(1, PARTS):
        to_all(sig_out.at[part], sig_in.at[part], 2 + part)

    all_copies(spec_out, spec_in, recv_sems.at[1]).wait()
    own_spec.wait()
    sf[...] = spec_in[...].astype(jnp.float32)
    for part in range(PARTS):
        all_copies(sig_out.at[part], sig_in.at[part], recv_sems.at[2 + part]).wait()
        keep(sig_out.at[part], sig_in.at[part], 1 + part).wait()
        xs[...] = sig_in[part].astype(jnp.float32)
        transform(xs, sf, ys, tabs)
        conv_out[part] = ys[...].astype(jnp.bfloat16)
        keep(conv_out.at[part], conv_in.at[part], 1 + PARTS + part).start()
        to_all(conv_out.at[part], conv_in.at[part], 2 + PARTS + part)

    @pl.loop(0, blocks)
    def _(block):
        lanes = pl.ds(pl.multiple_of(block * COLS, COLS), COLS)
        out[:, lanes] = bias[:, lanes] * gated[:, lanes].astype(jnp.float32)

    all_copies(spec_out, spec_in, send_sems.at[1]).wait()
    for part in range(PARTS):
        all_copies(sig_out.at[part], sig_in.at[part], send_sems.at[2 + part]).wait()
    for part in range(PARTS):
        number = 2 + PARTS + part
        all_copies(conv_out.at[part], conv_in.at[part], send_sems.at[number]).wait()
        all_copies(conv_out.at[part], conv_in.at[part], recv_sems.at[number]).wait()
        keep(conv_out.at[part], conv_in.at[part], 1 + PARTS + part).wait()

    @pl.loop(0, blocks)
    def _(block):
        lanes = pl.ds(pl.multiple_of(block * COLS, COLS), COLS)
        pieces = [
            conv_in[part, pl.ds(block * per, per)].astype(jnp.float32)[:, None]
            for part in range(PARTS)
        ]
        conv = jnp.concatenate(pieces, axis=1).reshape(COLS, COLS)
        out[:, lanes] = q_keep[:, lanes] * (jnp.transpose(conv) + out[:, lanes])


def local(projected, conv_weight, bias, spectrum):
    group = lax.axis_size("context")
    rows, channels = projected.shape[1:]
    bf16, f32 = jnp.bfloat16, jnp.float32
    made = tables(group)
    vmem = pl.BlockSpec(memory_space=pltpu.VMEM)
    return pl.pallas_call(
        functools.partial(kernel, group),
        out_shape=jax.ShapeDtypeStruct((rows, channels), f32),
        in_specs=[vmem] * (4 + len(made)),
        out_specs=vmem,
        scratch_shapes=[
            pltpu.VMEM((8, channels), bf16),
            pltpu.VMEM((8, channels), bf16),
            pltpu.VMEM((rows, channels), f32),
            pltpu.VMEM((rows, channels), bf16),
            pltpu.VMEM((group, PIECE, COLS), f32),
            pltpu.VMEM((group, PIECE, COLS), f32),
            pltpu.VMEM((group, 4, COLS), f32),
            pltpu.VMEM((PARTS, group, PIECE, COLS), bf16),
            pltpu.VMEM((PARTS, group, PIECE, COLS), bf16),
            pltpu.VMEM((group, 4, COLS), bf16),
            pltpu.VMEM((group, 4, COLS), bf16),
            pltpu.VMEM((PARTS, group, PIECE, COLS), bf16),
            pltpu.VMEM((PARTS, group, PIECE, COLS), bf16),
            pltpu.SemaphoreType.DMA((2 + 2 * PARTS,)),
            pltpu.SemaphoreType.DMA((2 + 2 * PARTS,)),
            pltpu.SemaphoreType.DMA((1 + 2 * PARTS,)),
        ],
        compiler_params=pltpu.CompilerParams(collective_id=0, has_side_effects=True),
        name="hyena",
    )(projected, conv_weight, bias[None, :], spectrum, *made)


def solution(mesh):
    placed = (
        P(None, "context", "dp"),
        P(None, None, "dp"),
        P("dp"),
        P(None, "context", None, "dp"),
    )
    return jax.shard_map(
        local, mesh=mesh, in_specs=placed, out_specs=P("context", "dp"), check_vma=False
    )
```

```python
import functools

import jax
import jax.numpy as jnp
import numpy as np
from jax import lax
from jax.experimental import pallas as pl
from jax.experimental.pallas import tpu as pltpu
from jax.sharding import PartitionSpec as P

COLS = 128
SHARE = 16
PARTS = 4
PIECE = SHARE // PARTS
HALF = PIECE // 2


def tables(data_rows):
    grid_rows = 2 * data_rows
    fft_len = grid_rows * COLS
    c = np.concatenate([np.arange(0, grid_rows, 2), np.arange(1, grid_rows, 2)])
    a = np.arange(data_rows)
    b = np.arange(COLS)
    rows = 2.0 * np.pi * (np.outer(c, a) % grid_rows) / grid_rows
    cols = 2.0 * np.pi * (np.outer(b, b) % COLS) / COLS
    twist = 2.0 * np.pi * (np.outer(c, b) % fft_len) / fft_len
    rc, rs = np.cos(rows), np.sin(rows)
    cc, cs = np.cos(cols), np.sin(cols)
    first = np.block([[rc, rs], [-rs, rc]])
    mid = np.block([[cc, -cs], [cs, cc]])
    back = np.block([[cc, cs], [-cs, cc]])
    last = np.block([[rc.T, -rs.T], [rs.T, rc.T]]) / fft_len
    split = []
    for table in (first, mid, back, last):
        table = table.astype(np.float32)
        high = table.astype(jnp.bfloat16)
        split += [high, (table - high.astype(np.float32)).astype(jnp.bfloat16)]
    return split + [np.cos(twist).astype(np.float32), np.sin(twist).astype(np.float32)]


def mm(x, y):
    return jnp.dot(x, y, preferred_element_type=jnp.float32)


def transform(xs, sp, ys, tabs):
    fh, fl, mh, ml, bh, bl, lh, ll, tc_ref, ts_ref = tabs
    tc, ts = tc_ref[...], ts_ref[...]
    grid_rows = tc.shape[0]
    fr = jnp.concatenate([sp[:, 0, :], sp[:, 1, :]], axis=0)
    fi = jnp.concatenate([sp[:, 2, :], sp[:, 3, :]], axis=0)
    for h in range(0, HALF, 2):
        pair = [
            jnp.concatenate([xs[:, i, :], xs[:, i + HALF, :]], axis=0).astype(jnp.bfloat16)
            for i in (h, h + 1)
        ]
        x = jnp.concatenate(pair, axis=1)
        y = mm(fh[...], x) + mm(fl[...], x)
        turned = []
        for i in range(2):
            yr = y[:grid_rows, i * COLS : (i + 1) * COLS]
            yi = y[grid_rows:, i * COLS : (i + 1) * COLS]
            z = jnp.concatenate([yr * tc + yi * ts, yi * tc - yr * ts], axis=1)
            z = z.astype(jnp.bfloat16)
            g = mm(z, mh[...]) + mm(z, ml[...])
            gr, gi = g[:, :COLS], g[:, COLS:]
            p = jnp.concatenate([gr * fr - gi * fi, gr * fi + gi * fr], axis=1)
            p = p.astype(jnp.bfloat16)
            q = mm(p, bh[...]) + mm(p, bl[...])
            qr, qi = q[:, :COLS], q[:, COLS:]
            turned.append(jnp.concatenate([qr * tc - qi * ts, qi * tc + qr * ts], axis=0))
        r = jnp.concatenate(turned, axis=1).astype(jnp.bfloat16)
        o = mm(lh[...], r) + mm(ll[...], r)
        n = grid_rows // 2
        for i in range(2):
            ys[:, h + i, :] = o[:n, i * COLS : (i + 1) * COLS]
            ys[:, h + i + HALF, :] = o[n:, i * COLS : (i + 1) * COLS]


def kernel(group, *refs):
    given = refs[:14]
    out = refs[14]
    loaded = refs[15:29]
    proj, weight, bias, spec = loaded[:4]
    tabs = loaded[4:]
    (load_sems, tail, halo, q_keep, gated, xs, ys, sf, sig_out, sig_in, spec_out, spec_in, conv_out, conv_in,
     send_sems, recv_sems, own_sems) = refs[29:]
    me = lax.axis_index("context")
    rows = proj.shape[1]
    blocks = proj.shape[2] // COLS
    per = COLS // SHARE

    def copy_to(src, dst, number, peer):
        return pltpu.make_async_remote_copy(
            src_ref=src,
            dst_ref=dst,
            send_sem=send_sems.at[number],
            recv_sem=recv_sems.at[number],
            device_id={"context": peer},
            device_id_type=pl.DeviceIdType.MESH,
        )

    def all_copies(src, dst, sem):
        some = pl.ds(0, group - 1)
        return pltpu.make_async_copy(src.at[some], dst.at[some], sem)

    def keep(src, dst, number):
        return pltpu.make_async_copy(src.at[me], dst.at[me], own_sems.at[number])

    def to_all(src, dst, number):
        @pl.loop(1, group)
        def _(k):
            peer = lax.rem(me + k, group)
            copy_to(src.at[peer], dst.at[me], number, peer).start()

    halo[...] = jnp.zeros_like(halo)
    barrier = pltpu.get_barrier_semaphore()

    @pl.loop(1, group)
    def _(k):
        pl.semaphore_signal(
            barrier,
            inc=1,
            device_id={"context": lax.rem(me + k, group)},
            device_id_type=pl.DeviceIdType.MESH,
        )

    loads = [
        pltpu.make_async_copy(src, dst, load_sems.at[i])
        for i, (src, dst) in enumerate(zip(given, loaded))
    ]
    for load in loads:
        load.start()
    for load in loads[:4]:
        load.wait()
    ends = [proj[j, rows - 16 :, :].astype(jnp.float32)[14:16, :] for j in range(3)]
    ends.append(jnp.zeros_like(ends[0]))
    tail[...] = jnp.concatenate(ends, axis=0).astype(jnp.bfloat16)
    for i in range(2):
        for j in range(2):
            sf[:, 2 * i + j, :] = jnp.transpose(spec[i, j])
    spec_out[...] = sf[...].astype(jnp.bfloat16)
    row = lax.broadcasted_iota(jnp.int32, (rows, COLS), 0)

    def short(x, j, lanes, e2, e1):
        n = row[: x.shape[0]]
        x1 = jnp.where(n == 0, e1, pltpu.roll(x, 1, 0))
        x2 = jnp.where(n == 0, e2, jnp.where(n == 1, e1, pltpu.roll(x, 2, 0)))
        w = weight[j, :, lanes]
        return w[0:1] * x + w[1:2] * x1 + w[2:3] * x2

    @pl.loop(0, blocks)
    def _(block):
        lanes = pl.ds(pl.multiple_of(block * COLS, COLS), COLS)
        none = jnp.zeros((1, COLS), jnp.float32)
        q, k, v = [
            short(proj[j, :, lanes].astype(jnp.float32), j, lanes, none, none) for j in range(3)
        ]
        q_keep[:, lanes] = q
        gated[:, lanes] = (k * v).astype(jnp.bfloat16)

    for load in loads[4:]:
        load.wait()
    pl.semaphore_wait(barrier, group - 1)

    @pl.when(me < group - 1)
    def _():
        copy_to(tail, halo, 0, me + 1).start()

    own_spec = keep(spec_out, spec_in, 0)
    own_spec.start()

    to_all(spec_out, spec_in, 1)

    @pl.when(me > 0)
    def _():
        copy_to(tail, halo, 0, me).wait_recv()

    @pl.when(me < group - 1)
    def _():
        copy_to(tail, halo, 0, me).wait_send()

    def send_block(block):
        for i in range(per):
            peer = block * per + lax.rem(me + i, per)

            @pl.when(peer != me)
            def _():
                copy_to(sig_out.at[0, peer], sig_in.at[0, me], 2, peer).start()

    @pl.loop(0, blocks)
    def _(step):
        block = lax.rem(step + me // per, blocks)
        lanes = pl.ds(pl.multiple_of(block * COLS, COLS), COLS)
        edge = halo[:, lanes].astype(jnp.float32)
        q, k, v = [
            short(
                proj[j, 0:16, lanes].astype(jnp.float32),
                j,
                lanes,
                edge[2 * j : 2 * j + 1, :],
                edge[2 * j + 1 : 2 * j + 2, :],
            )
            for j in range(3)
        ]
        q_keep[0:16, lanes] = q
        gated[0:16, lanes] = (k * v).astype(jnp.bfloat16)
        turned = jnp.transpose(gated[:, lanes].astype(jnp.float32))
        turned = turned.reshape(per, PARTS, PIECE, COLS)
        for part in range(PARTS):
            sig_out[part, pl.ds(block * per, per)] = turned[:, part].astype(jnp.bfloat16)

        @pl.when(step > 0)
        def _():
            send_block(lax.rem(step + blocks - 1 + me // per, blocks))

    send_block(lax.rem(blocks - 1 + me // per, blocks))
    for part in range(PARTS):
        keep(sig_out.at[part], sig_in.at[part], 1 + part).start()
    for part in range(1, PARTS):
        to_all(sig_out.at[part], sig_in.at[part], 2 + part)

    all_copies(spec_out, spec_in, recv_sems.at[1]).wait()
    own_spec.wait()
    sf[...] = spec_in[...].astype(jnp.float32)
    for part in range(PARTS):
        all_copies(sig_out.at[part], sig_in.at[part], recv_sems.at[2 + part]).wait()
        keep(sig_out.at[part], sig_in.at[part], 1 + part).wait()
        xs[...] = sig_in[part].astype(jnp.float32)
        transform(xs, sf, ys, tabs)
        conv_out[part] = ys[...].astype(jnp.bfloat16)
        keep(conv_out.at[part], conv_in.at[part], 1 + PARTS + part).start()
        to_all(conv_out.at[part], conv_in.at[part], 2 + PARTS + part)

    @pl.loop(0, blocks)
    def _(block):
        lanes = pl.ds(pl.multiple_of(block * COLS, COLS), COLS)
        out[:, lanes] = bias[:, lanes] * gated[:, lanes].astype(jnp.float32)

    all_copies(spec_out, spec_in, send_sems.at[1]).wait()
    for part in range(PARTS):
        all_copies(sig_out.at[part], sig_in.at[part], send_sems.at[2 + part]).wait()
    for part in range(PARTS):
        number = 2 + PARTS + part
        all_copies(conv_out.at[part], conv_in.at[part], send_sems.at[number]).wait()
        all_copies(conv_out.at[part], conv_in.at[part], recv_sems.at[number]).wait()
        keep(conv_out.at[part], conv_in.at[part], 1 + PARTS + part).wait()

    @pl.loop(0, blocks)
    def _(block):
        lanes = pl.ds(pl.multiple_of(block * COLS, COLS), COLS)
        pieces = [
            conv_in[part, pl.ds(block * per, per)].astype(jnp.float32)[:, None]
            for part in range(PARTS)
        ]
        conv = jnp.concatenate(pieces, axis=1).reshape(COLS, COLS)
        out[:, lanes] = q_keep[:, lanes] * (jnp.transpose(conv) + out[:, lanes])


def local(projected, conv_weight, bias, spectrum):
    group = lax.axis_size("context")
    rows, channels = projected.shape[1:]
    bf16, f32 = jnp.bfloat16, jnp.float32
    made = tables(group)
    vmem = pl.BlockSpec(memory_space=pltpu.VMEM)
    given = (projected, conv_weight, bias[None, :], spectrum, *made)
    return pl.pallas_call(
        functools.partial(kernel, group),
        out_shape=jax.ShapeDtypeStruct((rows, channels), f32),
        in_specs=[pl.BlockSpec(memory_space=pl.ANY)] * len(given),
        out_specs=vmem,
        scratch_shapes=[pltpu.VMEM(x.shape, x.dtype) for x in given]
        + [
            pltpu.SemaphoreType.DMA((len(given),)),
            pltpu.VMEM((8, channels), bf16),
            pltpu.VMEM((8, channels), bf16),
            pltpu.VMEM((rows, channels), f32),
            pltpu.VMEM((rows, channels), bf16),
            pltpu.VMEM((group, PIECE, COLS), f32),
            pltpu.VMEM((group, PIECE, COLS), f32),
            pltpu.VMEM((group, 4, COLS), f32),
            pltpu.VMEM((PARTS, group, PIECE, COLS), bf16),
            pltpu.VMEM((PARTS, group, PIECE, COLS), bf16),
            pltpu.VMEM((group, 4, COLS), bf16),
            pltpu.VMEM((group, 4, COLS), bf16),
            pltpu.VMEM((PARTS, group, PIECE, COLS), bf16),
            pltpu.VMEM((PARTS, group, PIECE, COLS), bf16),
            pltpu.SemaphoreType.DMA((2 + 2 * PARTS,)),
            pltpu.SemaphoreType.DMA((2 + 2 * PARTS,)),
            pltpu.SemaphoreType.DMA((1 + 2 * PARTS,)),
        ],
        compiler_params=pltpu.CompilerParams(collective_id=0, has_side_effects=True),
        name="hyena",
    )(*given)


def solution(mesh):
    placed = (
        P(None, "context", "dp"),
        P(None, None, "dp"),
        P("dp"),
        P(None, "context", None, "dp"),
    )
    return jax.shard_map(
        local, mesh=mesh, in_specs=placed, out_specs=P("context", "dp"), check_vma=False
    )
```
